32 devices in a mesh: dp: 8 (over z, x), tensor: 4 (over y, core).
Axes of the slice: x: 2, y: 2, z: 4, core: 2. Of those that a mesh axis runs over, the one named last changes fastest.
Arguments:
- residual: float32 [4096, 1024], P(('dp', 'tensor')), may hold values from -6 to 6
- segments: int32 [8, 512], P('dp'), may hold values from 0 to 10, never falling along the last dimension, each value on 1 to 256 neighbouring positions
- norm_gain: float32 [1024], replicated, may hold values from 0.5 to 1.5
- in_gate: bfloat16 [1024, 2048], P('dp', 'tensor'), may hold values from -0.1875 to 0.1875
- in_value: bfloat16 [1024, 2048], P('dp', 'tensor'), may hold values from -0.1875 to 0.1875
- in_step: bfloat16 [1024, 32], P('dp', 'tensor'), may hold values from -0.1875 to 0.1875
- in_state: bfloat16 [1024, 256], P('dp'), may hold values from -0.1875 to 0.1875
- kernel_value: float32 [4, 2048], P(None, 'tensor'), may hold values from -3 to 3
- bias_value: float32 [2048], P('tensor'), may hold values from -1.5 to 1.5
- kernel_state: float32 [4, 256], replicated, may hold values from -3 to 3
- bias_state: float32 [256], replicated, may hold values from -1.5 to 1.5
- step_bias: float32 [32], P('tensor'), may hold values from -5 to -1
- log_decay: float32 [32], P('tensor'), may hold values from -1 to 2.5
- skip_gain: float32 [32], P('tensor'), may hold values from 0.5 to 1.5
- gate_gain: float32 [2048], P('tensor'), may hold values from 0.5 to 1.5
- out_proj: bfloat16 [1024, 2048], P('dp', 'tensor'), may hold values from -0.125 to 0.125
- cotangent: float32 [4096, 1024], P(('dp', 'tensor')), may hold values from -6 to 6
Outputs:
- layer_out: float32 [4096, 1024], P(('dp', 'tensor'))
- grad_input: float32 [4096, 1024], P(('dp', 'tensor'))
- grad_norm_gain: float32 [1024], replicated
- grad_in_gate: float32 [1024, 2048], P('dp', 'tensor')
- grad_in_value: float32 [1024, 2048], P('dp', 'tensor')
- grad_in_step: float32 [1024, 32], P('dp', 'tensor')
- grad_in_state: float32 [1024, 256], P('dp', 'tensor')
- grad_kernel_value: float32 [4, 2048], P(None, 'tensor')
- grad_bias_value: float32 [2048], P('tensor')
- grad_kernel_state: float32 [4, 256], replicated
- grad_bias_state: float32 [256], replicated
- grad_step_bias: float32 [32], P('tensor')
- grad_log_decay: float32 [32], P('tensor')
- grad_skip_gain: float32 [32], P('tensor')
- grad_gate_gain: float32 [2048], P('tensor')
- grad_out_proj: float32 [1024, 2048], P('dp', 'tensor')
The draws below stay inside these ranges and needn't reach their ends.
Inputs may be any that keep to these rules, and one draw needn't show every extreme that they name: `segments`: segment numbers start at 0 in each packed row and never fall along it; one segment of each row holds exactly 256 tokens, none more.
All inputs are finite; a program needn't handle non-finite values.
Results may differ from the reference program's by a relative error of at most 0.0083.
Values may be sent and summed in bfloat16 or wider, within the bound.
A program may use at most 128 MiB of HBM per device.

```python
import math
from functools import partial
import jax
import jax.numpy as jnp
import numpy as np
from jax import lax

D = 1024
HEADS = 32
NSTATE = 128
CONV = 4
BLOCK = 256
SEQ = 512
INNER = 2048
TOKENS = 4096
N_DP = 8


def block_levels(own_key, extent, shards, least, largest):
    factor_of, own = 1.0, jax.random.fold_in(own_key, 6)
    for dim, blocks in shards:
        draws = jnp.exp(jax.random.uniform(jax.random.fold_in(own, dim), (blocks,), jnp.float32, least / len(shards), largest / len(shards)))
        factor_of = factor_of * jnp.repeat(draws, extent[dim] // blocks).reshape([-1 if axis == dim else 1 for axis in range(len(extent))])
    return factor_of


def length_profile(number_of, total, bound, slope):
    weights = [(1 << 20) // math.isqrt(rank ** slope) + 1 for rank in range(2, number_of + 1)]
    surplus, counts = total - bound - (number_of - 1), [1] * (number_of - 1)
    while surplus > 0:
        candidates = [i for i in range(number_of - 1) if counts[i] < bound]
        mass, remaining = sum([weights[i] for i in candidates]), surplus
        for i in candidates:
            addition = min(bound - counts[i], max(1, remaining * weights[i] // mass), surplus)
            counts[i] = counts[i] + addition
            surplus = surplus - addition
    return np.array([bound] + counts)


def ragged(key, amount, total, bound, skew):
    if amount == 2:
        one = jax.random.randint(key, (), max(1, total - bound), min(bound, total - 1) + 1)
        return jnp.stack([one, total - one])
    tallies = jnp.asarray(length_profile(amount, total, bound, skew), jnp.int32)
    twos = (amount - 1) // 2
    source_of, receiver = tallies[1:1 + 2 * twos:2], tallies[2:2 + 2 * twos:2]
    margin = jnp.minimum(source_of - 1, bound - receiver)
    moved = jax.random.randint(jax.random.fold_in(key, 1), (twos,), 0, 1 << 20) % (margin + 1)
    tallies = tallies.at[1:1 + 2 * twos:2].set(source_of - moved).at[2:2 + 2 * twos:2].set(receiver + moved)
    return tallies[jax.random.permutation(jax.random.fold_in(key, 2), amount)]


def bell_draw(own_key, extent, scale, most, shards=(), kind=jnp.bfloat16):
    array = scale * jax.random.normal(own_key, extent, jnp.float32)
    if shards:
        array = array * block_levels(own_key, extent, shards, -0.22, 0.18)
    return jnp.clip(array, -most, most).astype(kind)


def setup_inputs(seed: int = 0) -> dict:
    seeds = jax.random.split(jax.random.key(seed), 18)
    residual = bell_draw(seeds[0], (TOKENS, D), 1.0, 6.0, ((0, 32),), jnp.float32)
    segments = jax.vmap(lambda own: jnp.searchsorted(jnp.cumsum(ragged(own, SEQ // 64 + 3, SEQ, SEQ // 2, 1)), jnp.arange(SEQ), side="right"))(jax.random.split(seeds[1], N_DP)).reshape((N_DP, SEQ)).astype(jnp.int32)
    norm_gain = jnp.clip(1.0 + 0.1 * jax.random.normal(seeds[2], (D,), jnp.float32), 0.5, 1.5)
    in_gate = bell_draw(seeds[3], (D, INNER), D ** -0.5, 0.1875, ((0, 8), (1, 4)))
    in_value = bell_draw(seeds[4], (D, INNER), D ** -0.5, 0.1875, ((0, 8), (1, 4)))
    in_step = bell_draw(seeds[5], (D, HEADS), D ** -0.5, 0.1875, ((0, 8), (1, 4)))
    in_state = bell_draw(seeds[6], (D, 2 * NSTATE), D ** -0.5, 0.1875, ((0, 8),))
    kernel_value = bell_draw(seeds[7], (CONV, INNER), CONV ** -0.5, 3.0, ((1, 4),), jnp.float32)
    bias_value = bell_draw(seeds[8], (INNER,), 0.3, 1.5, ((0, 4),), jnp.float32)
    kernel_state = bell_draw(seeds[9], (CONV, 2 * NSTATE), CONV ** -0.5, 3.0, (), jnp.float32)
    bias_state = bell_draw(seeds[10], (2 * NSTATE,), 0.3, 1.5, (), jnp.float32)
    step_bias = jnp.clip(-5.0 + 4.0 * jax.random.uniform(seeds[11], (HEADS,), jnp.float32) ** block_levels(seeds[11], (HEADS,), ((0, 4),), -0.2, 0.2), -5.0, -1.0)
    log_decay = jnp.clip(-1.0 + 3.5 * jax.random.uniform(seeds[12], (HEADS,), jnp.float32) ** block_levels(seeds[12], (HEADS,), ((0, 4),), -0.2, 0.2), -1.0, 2.5)
    skip_gain = jnp.clip(0.5 + 1.0 * jax.random.uniform(seeds[13], (HEADS,), jnp.float32) ** block_levels(seeds[13], (HEADS,), ((0, 4),), -0.2, 0.2), 0.5, 1.5)
    gate_gain = jnp.clip(1.0 + 0.1 * jax.random.normal(seeds[14], (INNER,), jnp.float32), 0.5, 1.5)
    out_proj = bell_draw(seeds[15], (D, INNER), INNER ** -0.5, 0.125, ((0, 8), (1, 4)))
    cotangent = bell_draw(seeds[16], (TOKENS, D), 1.0, 6.0, ((0, 32),), jnp.float32)
    return {"residual": residual, "segments": segments, "norm_gain": norm_gain, "in_gate": in_gate, "in_value": in_value, "in_step": in_step, "in_state": in_state, "kernel_value": kernel_value, "bias_value": bias_value, "kernel_state": kernel_state, "bias_state": bias_state, "step_bias": step_bias, "log_decay": log_decay, "skip_gain": skip_gain, "gate_gain": gate_gain, "out_proj": out_proj, "cotangent": cotangent}


epsilon = 1e-05
precise = lax.Precision.HIGHEST

def pre_norm(row_block, gain):
    return row_block * lax.rsqrt(lax.optimization_barrier(jnp.mean(row_block * row_block, axis=1, keepdims=True)) + epsilon) * gain

def gated_norm(mixer_out, gate_raw, gain):
    gated_vals = mixer_out * jax.nn.silu(gate_raw)
    return gated_vals * lax.rsqrt(lax.optimization_barrier(jnp.mean(gated_vals * gated_vals, axis=1, keepdims=True)) + epsilon) * gain

def conv_silu(values, kernel, shift_bias, seg_ids):
    taps = kernel.shape[0]
    length = values.shape[0]
    padded = jnp.pad(values, ((taps - 1, 0), (0, 0)))
    seg_pad = jnp.concatenate([jnp.full((taps - 1,), -1, jnp.int32), seg_ids.astype(jnp.int32)])
    summed = jnp.zeros_like(values) + shift_bias
    for offset in range(taps):
        begin_at = taps - 1 - offset
        shifted = padded[begin_at:begin_at + length]
        same_doc = (seg_pad[begin_at:begin_at + length] == seg_ids).astype(values.dtype)
        summed = summed + kernel[offset] * shifted * same_doc[:, None]
    return jax.nn.silu(summed)

def ssd_mixer(values, write_vec, read_vec, step_raw, step_bias, log_decay, skip_gain, seg_ids):
    length, channels = values.shape
    head_count = step_raw.shape[1]
    head_size = channels // head_count
    states = write_vec.shape[1]
    blocks = length // BLOCK
    step_size = jax.nn.softplus(step_raw + step_bias)
    log_keep = -jnp.exp(log_decay) * step_size
    val_blocks = values.reshape(blocks, BLOCK, head_count, head_size)
    write_blocks = write_vec.reshape(blocks, BLOCK, states)
    read_blocks = read_vec.reshape(blocks, BLOCK, states)
    step_blocks = step_size.reshape(blocks, BLOCK, head_count)
    keep_blocks = log_keep.reshape(blocks, BLOCK, head_count)
    seg_blocks = seg_ids.astype(jnp.int32).reshape(blocks, BLOCK)
    carried = jnp.concatenate([jnp.full((1,), -1, jnp.int32), seg_blocks[:-1, -1]])
    row_pos = lax.broadcasted_iota(jnp.int32, (BLOCK, BLOCK), 0)
    col_pos = lax.broadcasted_iota(jnp.int32, (BLOCK, BLOCK), 1)

    def advance(carry_state, block_item):
        val_b, write_b, read_b, step_b, keep_b, seg_b, prior_seg = block_item
        cumulative = jnp.cumsum(keep_b, axis=0).T
        allowed = ((seg_b[:, None] == seg_b[None, :]) & (col_pos <= row_pos))[None]
        spread = cumulative[:, :, None] - cumulative[:, None, :]
        decay_mask = jnp.where(allowed, jnp.exp(jnp.where(allowed, spread, 0.0)), 0.0)
        scores = jnp.dot(read_b, write_b.T, precision=precise)
        mixing = scores[None] * decay_mask * step_b.T[:, None, :]
        inner_part = jnp.einsum('hls,shp->lhp', mixing, val_b, precision=precise)
        keep_prior = (seg_b == prior_seg).astype(values.dtype)
        from_state = jnp.einsum('ln,hpn->lhp', read_b, carry_state, precision=precise)
        carry_scale = jnp.exp(cumulative).T * keep_prior[:, None]
        outer_part = from_state * carry_scale[:, :, None]
        last_seg = seg_b[-1]
        tail_weight = jnp.exp(cumulative[:, -1][None, :] - cumulative.T) * step_b * (seg_b == last_seg).astype(values.dtype)[:, None]
        weighted = val_b * tail_weight[:, :, None]
        fresh_state = jnp.einsum('shp,sn->hpn', weighted, write_b, precision=precise)
        kept_scale = jnp.exp(cumulative[:, -1]) * (last_seg == prior_seg).astype(values.dtype)
        new_state = carry_state * kept_scale[:, None, None] + fresh_state
        return (new_state, inner_part + outer_part)
    initial = jnp.zeros((head_count, head_size, states), values.dtype)
    unused_state, outputs = lax.scan(advance, initial, (val_blocks, write_blocks, read_blocks, step_blocks, keep_blocks, seg_blocks, carried))
    return outputs.reshape(length, channels) + values * jnp.repeat(skip_gain, head_size)[None, :]

def reference(residual, segments, norm_gain, in_gate, in_value, in_step, in_state, kernel_value, bias_value, kernel_state, bias_state, step_bias, log_decay, skip_gain, gate_gain, out_proj, cotangent):
    in_cat = jnp.concatenate([in_gate, in_value, in_step, in_state], axis=1)
    rows_all = residual.reshape(N_DP, SEQ, D)
    cot_all = cotangent.reshape(N_DP, SEQ, D)
    split_one = 2 * INNER
    split_two = 2 * INNER + HEADS

    def one_row(totals, row_item):
        row_block, seg_ids, cot_block = row_item
        normed32, norm_pull = jax.vjp(pre_norm, row_block, norm_gain)
        normed = normed32.astype(jnp.bfloat16)
        projected = jnp.dot(normed, in_cat, preferred_element_type=jnp.float32)
        gate_raw = projected[:, :INNER]
        value_raw = projected[:, INNER:split_one]
        step_raw = projected[:, split_one:split_two]
        state_raw = projected[:, split_two:]
        conv_value, value_pull = jax.vjp(partial(conv_silu, seg_ids=seg_ids), value_raw, kernel_value, bias_value)
        conv_state, state_pull = jax.vjp(partial(conv_silu, seg_ids=seg_ids), state_raw, kernel_state, bias_state)
        mixer_out, mixer_pull = jax.vjp(partial(ssd_mixer, seg_ids=seg_ids), conv_value, conv_state[:, :NSTATE], conv_state[:, NSTATE:], step_raw, step_bias, log_decay, skip_gain)
        gate_out, gate_pull = jax.vjp(gated_norm, mixer_out, gate_raw, gate_gain)
        gate_normed = gate_out.astype(jnp.bfloat16)
        layer_rows = row_block + lax.dot_general(gate_normed, out_proj, (((1,), (1,)), ((), ())), preferred_element_type=jnp.float32)
        cot_half = cot_block.astype(jnp.bfloat16)
        grad_gate_normed = jnp.dot(cot_half, out_proj, preferred_element_type=jnp.float32)
        grad_out = lax.dot_general(cot_half, gate_normed, (((0,), (0,)), ((), ())), preferred_element_type=jnp.float32)
        grad_mixer_out, grad_gate_raw, grad_gate_gain = gate_pull(grad_gate_normed)
        grad_conv_value, grad_write, grad_read, grad_step_raw, grad_step_bias, grad_log_decay, grad_skip = mixer_pull(grad_mixer_out)
        grad_value_raw, grad_kernel_value, grad_bias_value = value_pull(grad_conv_value)
        grad_state_raw, grad_kernel_state, grad_bias_state = state_pull(jnp.concatenate([grad_write, grad_read], axis=1))
        grad_projected = jnp.concatenate([grad_gate_raw, grad_value_raw, grad_step_raw, grad_state_raw], axis=1).astype(jnp.bfloat16)
        grad_normed = lax.dot_general(grad_projected, in_cat, (((1,), (1,)), ((), ())), preferred_element_type=jnp.float32)
        grad_weights = lax.dot_general(normed, grad_projected, (((0,), (0,)), ((), ())), preferred_element_type=jnp.float32)
        grad_rows, grad_norm_part = norm_pull(grad_normed)
        grad_in_rows = cot_block + grad_rows
        updates = (grad_norm_part, grad_weights, grad_kernel_value, grad_bias_value, grad_kernel_state, grad_bias_state, grad_step_bias, grad_log_decay, grad_skip, grad_gate_gain, grad_out)
        totals = jax.tree.map(lambda running, update_term: running + update_term, totals, updates)
        return (totals, (layer_rows, grad_in_rows))
    initial = (jnp.zeros((D,), jnp.float32), jnp.zeros((D, 2 * INNER + HEADS + 2 * NSTATE), jnp.float32), jnp.zeros((CONV, INNER), jnp.float32), jnp.zeros((INNER,), jnp.float32), jnp.zeros((CONV, 2 * NSTATE), jnp.float32), jnp.zeros((2 * NSTATE,), jnp.float32), jnp.zeros((HEADS,), jnp.float32), jnp.zeros((HEADS,), jnp.float32), jnp.zeros((HEADS,), jnp.float32), jnp.zeros((INNER,), jnp.float32), jnp.zeros((D, INNER), jnp.float32))
    totals, outputs = lax.scan(one_row, initial, (rows_all, segments, cot_all))
    layer_out = outputs[0].reshape(TOKENS, D)
    grad_input = outputs[1].reshape(TOKENS, D)
    grad_weights = totals[1]
    return (layer_out, grad_input, totals[0], grad_weights[:, :INNER], grad_weights[:, INNER:split_one], grad_weights[:, split_one:split_two], grad_weights[:, split_two:], totals[2], totals[3], totals[4], totals[5], totals[6], totals[7], totals[8], totals[9], totals[10])
```

```python
from functools import partial

import jax
import jax.numpy as jnp
from jax import lax
from jax.experimental import pallas as pl
from jax.experimental.pallas import tpu as pltpu
from jax.sharding import PartitionSpec as P

epsilon = 1e-05
precise = lax.Precision.HIGHEST
MESH = pl.DeviceIdType.MESH
VM = pl.BlockSpec(memory_space=pltpu.VMEM)
F32 = jnp.float32
BF16 = jnp.bfloat16


def loop(begin, end, step):
    def body(k, carry):
        step(k)
        return carry

    lax.fori_loop(begin, end, body, 0)


def halves(cols):
    left = (cols // 128 + 1) // 2 * 128
    return pl.ds(0, left), pl.ds(left, cols - left)


def dev(d, t):
    return (d, t)


def push(src, dst, ssem, rsem, d, t):
    return pltpu.make_async_remote_copy(
        src_ref=src,
        dst_ref=dst,
        send_sem=ssem,
        recv_sem=rsem,
        device_id=dev(d, t),
        device_id_type=MESH,
    )


def greet_tensor(t_size, barrier):
    d = lax.axis_index("dp")
    t = lax.axis_index("tensor")
    for k in range(1, t_size):
        pl.semaphore_signal(
            barrier, inc=1, device_id=dev(d, lax.rem(t + k, t_size)), device_id_type=MESH
        )


def greet_dp(n, barrier):
    d = lax.axis_index("dp")
    t = lax.axis_index("tensor")

    def signal(k):
        pl.semaphore_signal(
            barrier, inc=1, device_id=dev(lax.rem(d + k, n), t), device_id_type=MESH
        )

    loop(1, n, signal)


def gather_kernel(
    n, t_size, a_ref, c_ref, w_ref, ga, gc, gw, sa, ra, sc, rc, sx, su, sd, rw
):
    d = lax.axis_index("dp")
    t = lax.axis_index("tensor")
    hi = d // 2
    lo = lax.rem(d, 2)
    line = n // 2
    parts = halves(w_ref.shape[1])
    everything = pl.ds(0, w_ref.shape[0])
    barrier = pltpu.get_barrier_semaphore()
    greet_tensor(t_size, barrier)
    greet_dp(n, barrier)
    pl.semaphore_wait(barrier, n + t_size - 2)
    mate = d + 1 - 2 * lo

    def at(h):
        return everything, parts[h]

    def own(h, sems, to):
        return push(w_ref.at[at(h)], gw.at[(d,) + at(h)], sems.at[h, d], rw.at[h, d], to, t)

    def relay(h, q, sems, to):
        return push(
            gw.at[(q,) + at(h)], gw.at[(q,) + at(h)], sems.at[h, q], rw.at[h, q], to, t
        )

    def arrive(h, q):
        push(
            gw.at[(q,) + at(h)], gw.at[(q,) + at(h)], sx.at[h, q], rw.at[h, q], mate, t
        ).wait_recv()

    has_up = hi < line - 1
    has_down = hi > 0
    own(0, sx, mate).start()
    for k in range(1, t_size):
        other = lax.rem(t + k, t_size)
        push(a_ref, ga.at[t], sa.at[other], ra.at[t], d, other).start()

    @pl.when(has_up)
    def _():
        own(1, su, d + 2).start()
        own(0, su, d + 2).start()

    @pl.when(has_down)
    def _():
        own(1, sd, d - 2).start()
        own(0, sd, d - 2).start()

    own(1, sx, mate).start()
    for k in range(1, t_size):
        other = lax.rem(t + k, t_size)
        push(c_ref, gc.at[t], sc.at[other], rc.at[t], d, other).start()
    gw[d] = w_ref[...]
    ga[t] = a_ref[...]
    gc[t] = c_ref[...]
    arrive(0, mate)

    @pl.when(has_up)
    def _():
        relay(0, mate, su, d + 2).start()

    @pl.when(has_down)
    def _():
        relay(0, mate, sd, d - 2).start()

    def step(k):
        for below in (True, False):
            far = d - 2 * k if below else d + 2 * k
            far_mate = mate - 2 * k if below else mate + 2 * k
            exists = hi >= k if below else hi + k < line
            onward = jnp.logical_and(exists, has_up if below else has_down)
            sems = su if below else sd
            to = d + 2 if below else d - 2

            @pl.when(exists)
            def _():
                arrive(1, far)
                relay(1, far, sx, mate).start()

            @pl.when(onward)
            def _():
                relay(1, far, sems, to).start()

            for q in (far, far_mate):

                @pl.when(exists)
                def _():
                    arrive(0, q)

                @pl.when(onward)
                def _():
                    relay(0, q, sems, to).start()

    loop(1, line, step)
    own(0, sx, mate).wait_send()

    def finish(k):
        arrive(1, 2 * k + 1 - lo)
        relay(1, 2 * k + lo, sx, mate).wait_send()

        @pl.when(jnp.logical_and(has_up, hi >= k))
        def _():
            relay(1, 2 * k + lo, su, mate).wait_send()
            for j in range(2):
                relay(0, 2 * k + j, su, mate).wait_send()

        @pl.when(jnp.logical_and(has_down, hi <= k))
        def _():
            relay(1, 2 * k + lo, sd, mate).wait_send()
            for j in range(2):
                relay(0, 2 * k + j, sd, mate).wait_send()

    loop(0, line, finish)
    for k in range(1, t_size):
        other = lax.rem(t + k, t_size)
        push(a_ref, ga.at[other], sa.at[other], ra.at[other], d, other).wait()
        push(c_ref, gc.at[other], sc.at[other], rc.at[other], d, other).wait()


def gather_all(n, t_size, a, c, w):
    dma = pltpu.SemaphoreType.DMA
    return pl.pallas_call(
        partial(gather_kernel, n, t_size),
        out_shape=(
            jax.ShapeDtypeStruct((t_size,) + a.shape, a.dtype),
            jax.ShapeDtypeStruct((t_size,) + c.shape, c.dtype),
            jax.ShapeDtypeStruct((n,) + w.shape, w.dtype),
        ),
        in_specs=[VM] * 3,
        out_specs=(VM, VM, VM),
        scratch_shapes=[dma((t_size,))] * 4 + [dma((2, n))] * 4,
        compiler_params=pltpu.CompilerParams(collective_id=0, has_side_effects=True),
    )(a, c, w)


def spread_kernel(t_size, scatter, x_ref, out_ref, ss, rs):
    d = lax.axis_index("dp")
    t = lax.axis_index("tensor")
    barrier = pltpu.get_barrier_semaphore()
    greet_tensor(t_size, barrier)
    pl.semaphore_wait(barrier, t_size - 1)
    for k in range(1, t_size):
        other = lax.rem(t + k, t_size)
        src = x_ref.at[other] if scatter else x_ref
        push(src, out_ref.at[t], ss.at[other], rs.at[t], d, other).start()
    out_ref[t] = x_ref[t] if scatter else x_ref[...]
    for k in range(1, t_size):
        other = lax.rem(t + k, t_size)
        src = x_ref.at[other] if scatter else x_ref
        push(src, out_ref.at[other], ss.at[other], rs.at[other], d, other).wait()


def spread_tensor(t_size, x, scatter, cid):
    dma = pltpu.SemaphoreType.DMA
    shape = x.shape if scatter else (t_size,) + x.shape
    return pl.pallas_call(
        partial(spread_kernel, t_size, scatter),
        out_shape=jax.ShapeDtypeStruct(shape, x.dtype),
        in_specs=[VM],
        out_specs=VM,
        scratch_shapes=[dma((t_size,))] * 2,
        compiler_params=pltpu.CompilerParams(collective_id=cid, has_side_effects=True),
    )(x)


def reduce_kernel(
    n,
    t_size,
    w_ref,
    l_ref,
    g_ref,
    res_ref,
    gain_ref,
    cot_ref,
    sd_ref,
    st_ref,
    w_out,
    l_out,
    gi_out,
    sd_out,
    st_out,
    rl,
    rg,
    rx0,
    rx1,
    ru1,
    rd1,
    ru0,
    rd0,
    bu1,
    bd1,
    bu0,
    bd0,
    bx1,
    st_mine,
    rst,
    st_sum,
    rst_dp,
    rsd,
    s_l,
    q_l,
    s_g,
    q_g,
    s_x0,
    q_x0,
    s_x1,
    q_x1,
    s_u1,
    q_u1,
    s_d1,
    q_d1,
    s_u0,
    q_u0,
    s_d0,
    q_d0,
    s_st,
    q_st,
    s_sp,
    q_sp,
    s_sd,
    q_sd,
):
    d = lax.axis_index("dp")
    t = lax.axis_index("tensor")
    hi = d // 2
    lo = lax.rem(d, 2)
    line = n // 2
    mate = d + 1 - 2 * lo
    rows = w_ref.shape[1]
    every = pl.ds(0, rows)
    top, low = halves(w_ref.shape[2])
    barrier = pltpu.get_barrier_semaphore()
    greet_tensor(t_size, barrier)
    greet_dp(n, barrier)
    pl.semaphore_wait(barrier, n + t_size - 2)
    has_up = hi < line - 1
    has_down = hi > 0

    def send_x0(k):
        return push(
            w_ref.at[2 * k + 1 - lo, every, top], rx0.at[k], s_x0.at[k], q_x0.at[k], mate, t
        )

    loop(0, line, lambda k: send_x0(k).start())

    def tensor_send(src, buf, ss, qs, other):
        return push(src.at[other], buf.at[t], ss.at[other], qs.at[t], d, other)

    for k in range(1, t_size):
        other = lax.rem(t + k, t_size)
        tensor_send(g_ref, rg, s_g, q_g, other).start()

    def sd_send(q):
        return push(sd_ref, rsd.at[d], s_sd.at[q], q_sd.at[d], q, t)

    loop(1, n, lambda k: sd_send(lax.rem(d + k, n)).start())
    for k in range(1, t_size):
        other = lax.rem(t + k, t_size)
        tensor_send(l_ref, rl, s_l, q_l, other).start()

    def hop(buf, got, ss, qs, k, to):
        return push(buf.at[k], got.at[k], ss.at[k], qs.at[k], to, t)

    def chain(k, mine, up):
        has_prev = has_down if up else has_up
        buf, got, ss, qs, to = (
            (mine[1], mine[2], mine[3], mine[4], d + 2)
            if up
            else (mine[5], mine[6], mine[7], mine[8], d - 2)
        )

        @pl.when(k > hi if up else k < hi)
        def _():
            @pl.when(has_prev)
            def _():
                hop(buf, got, ss, qs, k, to).wait_recv()
                buf[k] = (mine[0](k) + got[k].astype(F32)).astype(BF16)

            @pl.when(jnp.logical_not(has_prev))
            def _():
                buf[k] = mine[0](k).astype(BF16)

            hop(buf, got, ss, qs, k, to).start()

    def pair(k):
        return w_ref[pl.ds(2 * k, 2), :, low].astype(F32)

    set1 = (pair, bu1, ru1, s_u1, q_u1, bd1, rd1, s_d1, q_d1)

    def joined(k):
        return w_ref[2 * k + lo, :, top].astype(F32) + rx0[k].astype(F32)

    set0 = (joined, bu0, ru0, s_u0, q_u0, bd0, rd0, s_d0, q_d0)

    def walk1(k):
        chain(line - 1 - k, set1, True)
        chain(k, set1, False)

    loop(0, line - 1, walk1)

    g_sum = g_ref[t].astype(F32)
    for k in range(1, t_size):
        other = lax.rem(t + k, t_size)
        push(g_ref.at[other], rg.at[other], s_g.at[other], q_g.at[other], d, other).wait()
        g_sum = g_sum + rg[other].astype(F32)
    res = res_ref[...]
    inv = lax.rsqrt(jnp.mean(res * res, axis=1, keepdims=True) + epsilon)
    unit = res * inv
    scaled = g_sum * gain_ref[...]
    inner = jnp.mean(scaled * unit, axis=1, keepdims=True)
    gi_out[...] = cot_ref[...] + inv * (scaled - unit * inner)
    st_mine[...] = st_ref[...]
    st_mine[0:1] = jnp.sum(g_sum * unit, axis=0, keepdims=True)

    def st_send(other):
        return push(st_mine, rst.at[t], s_st.at[other], q_st.at[t], d, other)

    for k in range(1, t_size):
        st_send(lax.rem(t + k, t_size)).start()

    loop(
        0,
        line,
        lambda k: push(rx0.at[k], rx0.at[k], s_x0.at[k], q_x0.at[k], mate, t).wait_recv(),
    )

    def walk0(k):
        chain(line - 1 - k, set0, True)
        chain(k, set0, False)

    loop(0, line - 1, walk0)

    w_out[:, low] = w_ref[d, :, low].astype(F32)
    bx1[...] = w_ref[mate, :, low]

    @pl.when(has_down)
    def _():
        hop(bu1, ru1, s_u1, q_u1, hi, d).wait_recv()
        w_out[:, low] = w_out[:, low] + ru1[hi, lo].astype(F32)
        bx1[...] = (bx1[...].astype(F32) + ru1[hi, 1 - lo].astype(F32)).astype(BF16)

    @pl.when(has_up)
    def _():
        hop(bd1, rd1, s_d1, q_d1, hi, d).wait_recv()
        w_out[:, low] = w_out[:, low] + rd1[hi, lo].astype(F32)
        bx1[...] = (bx1[...].astype(F32) + rd1[hi, 1 - lo].astype(F32)).astype(BF16)

    send_x1 = push(bx1, rx1, s_x1.at[0], q_x1.at[0], mate, t)
    send_x1.start()

    st_total = st_mine[...]
    for k in range(1, t_size):
        other = lax.rem(t + k, t_size)
        push(st_mine, rst.at[other], s_st.at[other], q_st.at[other], d, other).wait()
        st_total = st_total + rst[other]
    st_sum[...] = st_total

    def sp_send(q):
        return push(st_sum, rst_dp.at[d], s_sp.at[q], q_sp.at[d], q, t)

    loop(1, n, lambda k: sp_send(lax.rem(d + k, n)).start())

    l_sum = l_ref[t].astype(F32)
    for k in range(1, t_size):
        other = lax.rem(t + k, t_size)
        push(l_ref.at[other], rl.at[other], s_l.at[other], q_l.at[other], d, other).wait()
        l_sum = l_sum + rl[other].astype(F32)
    l_out[...] = res_ref[...] + l_sum

    w_out[:, top] = joined(hi)

    @pl.when(has_down)
    def _():
        hop(bu0, ru0, s_u0, q_u0, hi, d).wait_recv()
        w_out[:, top] = w_out[:, top] + ru0[hi].astype(F32)

    @pl.when(has_up)
    def _():
        hop(bd0, rd0, s_d0, q_d0, hi, d).wait_recv()
        w_out[:, top] = w_out[:, top] + rd0[hi].astype(F32)

    send_x1.wait()
    w_out[:, low] = w_out[:, low] + rx1[...].astype(F32)

    rsd[d] = sd_ref[...]
    rst_dp[d] = st_sum[...]

    def settle(k):
        q = lax.rem(d + k, n)
        push(sd_ref, rsd.at[q], s_sd.at[q], q_sd.at[q], q, t).wait()
        push(st_sum, rst_dp.at[q], s_sp.at[q], q_sp.at[q], q, t).wait()

    loop(1, n, settle)
    sd_out[...] = jnp.sum(rsd[...], axis=0)
    st_out[...] = jnp.sum(rst_dp[...], axis=0)

    def drain(k):
        send_x0(k).wait_send()

        @pl.when(k > hi)
        def _():
            hop(bu1, ru1, s_u1, q_u1, k, d).wait_send()
            hop(bu0, ru0, s_u0, q_u0, k, d).wait_send()

        @pl.when(k < hi)
        def _():
            hop(bd1, rd1, s_d1, q_d1, k, d).wait_send()
            hop(bd0, rd0, s_d0, q_d0, k, d).wait_send()

    loop(0, line, drain)


def reduce_all(n, t_size, w, l, g, res, gain, cot, small_d, small_t):
    dma = pltpu.SemaphoreType.DMA
    vm = pltpu.VMEM
    rows, cols = w.shape[1:]
    line = n // 2
    left = halves(cols)[0].size
    two = vm((line, 2, rows, cols - left), BF16)
    one = vm((line, rows, left), BF16)
    tok = vm(l.shape, BF16)
    struct = jax.ShapeDtypeStruct
    t_sem = dma((t_size,))
    k_sem = dma((line,))
    n_sem = dma((n,))
    return pl.pallas_call(
        partial(reduce_kernel, n, t_size),
        out_shape=(
            struct((rows, cols), F32),
            struct(res.shape, F32),
            struct(res.shape, F32),
            struct(small_d.shape, F32),
            struct(small_t.shape, F32),
        ),
        in_specs=[VM] * 8,
        out_specs=(VM,) * 5,
        scratch_shapes=[
            tok,
            tok,
            one,
            vm((rows, cols - left), BF16),
            two,
            two,
            one,
            one,
            two,
            two,
            one,
            one,
            vm((rows, cols - left), BF16),
            vm(small_t.shape, F32),
            vm((t_size,) + small_t.shape, F32),
            vm(small_t.shape, F32),
            vm((n,) + small_t.shape, F32),
            vm((n,) + small_d.shape, F32),
        ]
        + [t_sem] * 4
        + [k_sem] * 2
        + [dma((1,))] * 2
        + [k_sem] * 8
        + [t_sem] * 2
        + [n_sem] * 4,
        compiler_params=pltpu.CompilerParams(collective_id=3, has_side_effects=True),
    )(w, l, g, res, gain, cot, small_d, small_t)


def dot_f(a, b, dims, precision=None):
    return lax.dot_general(
        a, b, ((dims[0], dims[1]), ((), ())), preferred_element_type=F32, precision=precision
    )


def decay_of(cum_col, cum_row, allowed):
    return jnp.where(allowed, jnp.exp(jnp.where(allowed, cum_col - cum_row, 0.0)), 0.0)


def allowed_of(seg_col, seg_row):
    size = seg_col.shape[0]
    row_pos = lax.broadcasted_iota(jnp.int32, (size, size), 0)
    col_pos = lax.broadcasted_iota(jnp.int32, (size, size), 1)
    return (seg_col == seg_row) & (col_pos <= row_pos)


def pick(ref, head):
    lanes = lax.broadcasted_iota(jnp.int32, ref.shape, 1)
    return jnp.sum(jnp.where(lanes == head, ref[...], 0.0), axis=1, keepdims=True)


def mix_kernel(
    width, x_ref, b_ref, c_ref, cum_ref, cumt_ref, step_ref, skip_ref, sc_ref, sr_ref, y_ref, scores
):
    j = pl.program_id(0)
    allowed = allowed_of(sc_ref[...], sr_ref[...])

    @pl.when(j == 0)
    def _():
        scores[...] = dot_f(c_ref[...], b_ref[...], ((1,), (1,)), precise)

    count = x_ref.shape[1] // width
    for i in range(count):
        head = j * count + i
        x = x_ref[:, i * width : (i + 1) * width]
        decay = decay_of(pick(cum_ref, head), cumt_ref[pl.ds(head, 1), :], allowed)
        mixing = (scores[...] * decay).astype(BF16)
        fed = (x * pick(step_ref, head)).astype(BF16)
        y = dot_f(mixing, fed, ((1,), (0,)))
        y_ref[:, i * width : (i + 1) * width] = y + pick(skip_ref, head) * x


def mix_forward(x, b, c, cum, step, skip, seg, width):
    tokens, channels = x.shape
    pairs = channels // 128
    whole = lambda a: pl.BlockSpec(a.shape, lambda j: (0,) * a.ndim)
    block = pl.BlockSpec((tokens, 128), lambda j: (0, j))
    args = (x, b, c, cum, cum.T, step, skip[None, :], seg[:, None], seg[None, :])
    return pl.pallas_call(
        partial(mix_kernel, width),
        grid=(pairs,),
        out_shape=jax.ShapeDtypeStruct(x.shape, F32),
        in_specs=[block] + [whole(a) for a in args[1:]],
        out_specs=block,
        scratch_shapes=[pltpu.VMEM((tokens, tokens), F32)],
    )(*args)


def back_kernel(
    width,
    x_ref,
    dy_ref,
    b_ref,
    c_ref,
    cum_ref,
    cumt_ref,
    step_ref,
    skip_ref,
    sc_ref,
    sr_ref,
    dx_ref,
    db_ref,
    dc_ref,
    row_ref,
    col_ref,
    dstep_ref,
    dskip_ref,
    scores,
    d_scores,
):
    j = pl.program_id(0)
    allowed = allowed_of(sc_ref[...], sr_ref[...])

    @pl.when(j == 0)
    def _():
        scores[...] = dot_f(c_ref[...], b_ref[...], ((1,), (1,)), precise)
        d_scores[...] = jnp.zeros_like(d_scores)
        row_ref[...] = jnp.zeros_like(row_ref)
        dstep_ref[...] = jnp.zeros_like(dstep_ref)
        dskip_ref[...] = jnp.zeros_like(dskip_ref)

    lanes = lax.broadcasted_iota(jnp.int32, row_ref.shape, 1)
    count = x_ref.shape[1] // width
    for i in range(count):
        head = j * count + i
        x = x_ref[:, i * width : (i + 1) * width]
        dy = dy_ref[:, i * width : (i + 1) * width]
        step = pick(step_ref, head)
        decay = decay_of(pick(cum_ref, head), cumt_ref[pl.ds(head, 1), :], allowed)
        mixing = scores[...] * decay
        fed = (x * step).astype(BF16)
        dy_half = dy.astype(BF16)
        d_mix = dot_f(dy_half, fed, ((1,), (1,)))
        d_fed = dot_f(mixing.astype(BF16), dy_half, ((0,), (0,)))
        d_scores[...] += d_mix * decay
        energy = d_mix * mixing
        hot = lanes == head
        row_ref[...] += jnp.where(hot, jnp.sum(energy, axis=1, keepdims=True), 0.0)
        col_ref[pl.ds(head, 1), :] = jnp.sum(energy, axis=0, keepdims=True)
        dstep_ref[...] += jnp.where(hot, jnp.sum(d_fed * x, axis=1, keepdims=True), 0.0)
        dskip_ref[...] += jnp.where(hot, jnp.sum(dy * x, axis=1, keepdims=True), 0.0)
        dx_ref[:, i * width : (i + 1) * width] = d_fed * step + pick(skip_ref, head) * dy

    @pl.when(j == pl.num_programs(0) - 1)
    def _():
        grad = d_scores[...].astype(BF16)
        dc_ref[...] = dot_f(grad, b_ref[...].astype(BF16), ((1,), (0,)))
        db_ref[...] = dot_f(grad, c_ref[...].astype(BF16), ((0,), (0,)))


def mix_backward(x, dy, b, c, cum, step, skip, seg, width):
    tokens, channels = x.shape
    heads = cum.shape[1]
    pairs = channels // 128
    whole = lambda a: pl.BlockSpec(a.shape, lambda j: (0,) * a.ndim)
    block = pl.BlockSpec((tokens, 128), lambda j: (0, j))
    struct = jax.ShapeDtypeStruct
    args = (x, dy, b, c, cum, cum.T, step, skip[None, :], seg[:, None], seg[None, :])
    outs = (
        struct(x.shape, F32),
        struct(b.shape, F32),
        struct(c.shape, F32),
        struct((tokens, heads), F32),
        struct((heads, tokens), F32),
        struct((tokens, heads), F32),
        struct((tokens, heads), F32),
    )
    return pl.pallas_call(
        partial(back_kernel, width),
        grid=(pairs,),
        out_shape=outs,
        in_specs=[block, block] + [whole(a) for a in args[2:]],
        out_specs=(block,) + tuple(whole(a) for a in outs[1:]),
        scratch_shapes=[pltpu.VMEM((tokens, tokens), F32)] * 2,
    )(*args)


def conv_silu(values, kernel, shift_bias, seg_ids):
    taps = kernel.shape[0]
    length = values.shape[0]
    padded = jnp.pad(values, ((taps - 1, 0), (0, 0)))
    seg_pad = jnp.concatenate([jnp.full((taps - 1,), -1, jnp.int32), seg_ids])
    summed = jnp.zeros_like(values) + shift_bias
    for offset in range(taps):
        begin_at = taps - 1 - offset
        shifted = padded[begin_at : begin_at + length]
        same_doc = (seg_pad[begin_at : begin_at + length] == seg_ids).astype(values.dtype)
        summed = summed + kernel[offset] * shifted * same_doc[:, None]
    return jax.nn.silu(summed)


def local(
    n,
    t_size,
    residual,
    segments,
    norm_gain,
    in_gate,
    in_value,
    in_step,
    in_state,
    kernel_value,
    bias_value,
    kernel_state,
    bias_state,
    step_bias,
    log_decay,
    skip_gain,
    gate_gain,
    out_proj,
    cotangent,
):
    seg_ids = segments[0]
    width = in_gate.shape[1]
    heads = in_step.shape[1]
    states = in_state.shape[1]
    model = residual.shape[1]
    inner = width * t_size
    rows = in_gate.shape[0]
    tokens = seg_ids.shape[0]
    t = lax.axis_index("tensor")

    inv = lax.rsqrt(jnp.mean(residual * residual, axis=1, keepdims=True) + epsilon)
    normed = (residual * inv * norm_gain).astype(BF16)
    cot_half = cotangent.astype(BF16)
    step_pad = -heads % 128
    w_mine = jnp.concatenate(
        [
            in_gate,
            in_value,
            in_state,
            in_step,
            jnp.zeros((rows, step_pad), BF16),
            out_proj,
        ],
        axis=1,
    )
    full_rows, cot_full, w_full = gather_all(n, t_size, normed, cot_half, w_mine)
    full_rows = full_rows.reshape(tokens, model)
    cot_full = cot_full.reshape(tokens, model)
    w_full = w_full.reshape(model, w_mine.shape[1])
    s1, s2 = 2 * width, 2 * width + states
    s3 = s2 + heads
    out_full = w_full[:, s3 + step_pad :]

    projected = jnp.dot(full_rows, w_full[:, : s3 + step_pad], preferred_element_type=F32)
    gate_raw = projected[:, :width]
    value_raw = projected[:, width:s1]
    state_raw = projected[:, s1:s2]
    step_raw = projected[:, s2:s3]
    conv_value, value_pull = jax.vjp(
        partial(conv_silu, seg_ids=seg_ids), value_raw, kernel_value, bias_value
    )
    conv_state = conv_silu(state_raw, kernel_state, bias_state, seg_ids)
    part = states // 2
    write_vec, read_vec = conv_state[:, :part], conv_state[:, part:]
    step_in = step_raw + step_bias
    step_size = jax.nn.softplus(step_in)
    rate = -jnp.exp(log_decay)
    log_keep = rate * step_size
    tri = jnp.tril(jnp.ones((tokens, tokens), F32))
    cum = jnp.dot(tri, log_keep, precision=precise)
    head_width = width // heads
    mixer_out = mix_forward(
        conv_value, write_vec, read_vec, cum, step_size, skip_gain, seg_ids, head_width
    )

    sig_gate = jax.nn.sigmoid(gate_raw)
    gate_act = gate_raw * sig_gate
    gated = mixer_out * gate_act
    grad_gate_normed = jnp.dot(cot_full, out_full, preferred_element_type=F32)
    scaled = grad_gate_normed * gate_gain
    sums = jnp.concatenate(
        [
            jnp.sum(gated * gated, axis=1).reshape(-1, 128),
            jnp.sum(scaled * gated, axis=1).reshape(-1, 128),
        ],
        axis=0,
    )
    totals = jnp.sum(spread_tensor(t_size, sums, False, 1), axis=0)
    split = tokens // 128
    total_sq = totals[:split].reshape(tokens)
    total_dot = totals[split:].reshape(tokens)
    inv_rms = lax.rsqrt(total_sq / inner + epsilon)[:, None]
    gate_normed = (gated * inv_rms * gate_gain).astype(BF16)
    grad_gate_gain = jnp.sum(grad_gate_normed * gated * inv_rms, axis=0)
    grad_gated = inv_rms * scaled - gated * inv_rms**3 * (total_dot / inner)[:, None]
    grad_mixer_out = grad_gated * gate_act
    grad_gate_raw = grad_gated * mixer_out * sig_gate * (1.0 + gate_raw * (1.0 - sig_gate))

    grad_conv_value, grad_b, grad_c, row_e, col_e, d_fed_step, d_skip = mix_backward(
        conv_value,
        grad_mixer_out,
        write_vec,
        read_vec,
        cum,
        step_size,
        skip_gain,
        seg_ids,
        head_width,
    )
    slice_width = states // t_size
    grad_bc = jnp.concatenate([grad_b, grad_c], axis=1).astype(BF16)
    pieces = grad_bc.reshape(tokens, t_size, slice_width).transpose(1, 0, 2)
    grad_conv_state = jnp.sum(
        spread_tensor(t_size, pieces, True, 2).astype(F32), axis=0
    )
    d_keep = lax.dot_general(
        tri, row_e - col_e.T, (((0,), (0,)), ((), ())), precision=precise
    )
    grad_step_raw = (d_fed_step + d_keep * rate) * jax.nn.sigmoid(step_in)
    grad_step_bias = jnp.sum(grad_step_raw, axis=0)
    grad_log_decay = jnp.sum(d_keep * log_keep, axis=0)
    grad_skip = jnp.sum(d_skip, axis=0)

    grad_value_raw, grad_kernel_value, grad_bias_value = value_pull(grad_conv_value)
    begin = t * slice_width
    unused, state_pull = jax.vjp(
        partial(conv_silu, seg_ids=seg_ids),
        lax.dynamic_slice_in_dim(state_raw, begin, slice_width, 1),
        lax.dynamic_slice_in_dim(kernel_state, begin, slice_width, 1),
        lax.dynamic_slice_in_dim(bias_state, begin, slice_width, 0),
    )
    grad_state_slice, grad_ks, grad_bs = state_pull(grad_conv_state)
    state_cols = lax.dynamic_slice_in_dim(w_full[:, s1:s2], begin, slice_width, 1)

    fill = -(slice_width + heads) % 128
    grad_projected = jnp.concatenate(
        [
            grad_gate_raw,
            grad_value_raw,
            grad_state_slice,
            grad_step_raw,
            jnp.zeros((tokens, fill), F32),
        ],
        axis=1,
    ).astype(BF16)
    back_cat = jnp.concatenate(
        [w_full[:, :s1], state_cols, w_full[:, s2:s3], jnp.zeros((model, fill), BF16)], axis=1
    )
    grad_normed = lax.dot_general(
        grad_projected, back_cat, (((1,), (1,)), ((), ())), preferred_element_type=F32
    ).astype(BF16)
    layer_part = lax.dot_general(
        gate_normed, out_full, (((1,), (1,)), ((), ())), preferred_element_type=F32
    ).astype(BF16)
    grad_weights = lax.dot_general(
        full_rows, grad_projected, (((0,), (0,)), ((), ())), preferred_element_type=F32
    ).astype(BF16)
    grad_out = lax.dot_general(
        cot_full, gate_normed, (((0,), (0,)), ((), ())), preferred_element_type=F32
    ).astype(BF16)
    grads = jnp.concatenate([grad_weights, grad_out], axis=1).reshape(n, rows, -1)

    misc = jnp.concatenate([grad_step_bias, grad_log_decay, grad_skip])
    misc = jnp.pad(misc, (0, width - misc.shape[0]))
    small_d = jnp.concatenate(
        [grad_kernel_value, grad_bias_value[None], grad_gate_gain[None], misc[None]], axis=0
    )
    small_d = jnp.pad(small_d, ((0, -small_d.shape[0] % 8), (0, 0)))
    taps = kernel_state.shape[0]
    state_grads = lax.dynamic_update_slice_in_dim(
        jnp.zeros((taps + 1, states), F32),
        jnp.concatenate([grad_ks, grad_bs[None]], axis=0),
        begin,
        1,
    )
    small_t = jnp.pad(state_grads, ((1, -(taps + 2) % 8), (0, model - states)))

    w_sum, layer_out, grad_input, sum_d, sum_t = reduce_all(
        n,
        t_size,
        grads,
        layer_part.reshape(t_size, -1, model),
        grad_normed.reshape(t_size, -1, model),
        residual,
        norm_gain[None],
        cotangent,
        small_d,
        small_t,
    )
    e1 = s1 + slice_width
    e2 = e1 + heads
    v_taps = kernel_value.shape[0]
    last = sum_d[v_taps + 2]
    return (
        layer_out,
        grad_input,
        sum_t[0],
        w_sum[:, :width],
        w_sum[:, width:s1],
        w_sum[:, e1:e2],
        w_sum[:, s1:e1],
        sum_d[:v_taps],
        sum_d[v_taps],
        sum_t[1 : taps + 1, :states],
        sum_t[taps + 1, :states],
        last[:heads],
        last[heads : 2 * heads],
        last[2 * heads : 3 * heads],
        sum_d[v_taps + 1],
        w_sum[:, e2 + fill :],
    )


def solution(mesh):
    in_specs = (
        P(("dp", "tensor"), None),
        P("dp", None),
        P(),
        P("dp", "tensor"),
        P("dp", "tensor"),
        P("dp", "tensor"),
        P("dp", None),
        P(None, "tensor"),
        P("tensor"),
        P(),
        P(),
        P("tensor"),
        P("tensor"),
        P("tensor"),
        P("tensor"),
        P("dp", "tensor"),
        P(("dp", "tensor"), None),
    )
    out_specs = (
        P(("dp", "tensor"), None),
        P(("dp", "tensor"), None),
        P(),
        P("dp", "tensor"),
        P("dp", "tensor"),
        P("dp", "tensor"),
        P("dp", "tensor"),
        P(None, "tensor"),
        P("tensor"),
        P(),
        P(),
        P("tensor"),
        P("tensor"),
        P("tensor"),
        P("tensor"),
        P("dp", "tensor"),
    )
    body = partial(local, mesh.shape["dp"], mesh.shape["tensor"])
    return jax.shard_map(body, mesh=mesh, in_specs=in_specs, out_specs=out_specs, check_vma=False)
```

```python
from functools import partial

import jax
import jax.numpy as jnp
from jax import lax
from jax.experimental import pallas as pl
from jax.experimental.pallas import tpu as pltpu
from jax.sharding import PartitionSpec as P

epsilon = 1e-05
precise = lax.Precision.HIGHEST
MESH = pl.DeviceIdType.MESH
VM = pl.BlockSpec(memory_space=pltpu.VMEM)
F32 = jnp.float32
BF16 = jnp.bfloat16


def loop(begin, end, step):
    def body(k, carry):
        step(k)
        return carry

    lax.fori_loop(begin, end, body, 0)


def halves(cols):
    left = cols // 128 * 2 // 5 * 128
    return pl.ds(0, left), pl.ds(left, cols - left)


def dev(d, t):
    return (d, t)


def push(src, dst, ssem, rsem, d, t):
    return pltpu.make_async_remote_copy(
        src_ref=src,
        dst_ref=dst,
        send_sem=ssem,
        recv_sem=rsem,
        device_id=dev(d, t),
        device_id_type=MESH,
    )


def greet_tensor(t_size, barrier):
    d = lax.axis_index("dp")
    t = lax.axis_index("tensor")
    for k in range(1, t_size):
        pl.semaphore_signal(
            barrier, inc=1, device_id=dev(d, lax.rem(t + k, t_size)), device_id_type=MESH
        )


def greet_dp(n, barrier):
    d = lax.axis_index("dp")
    t = lax.axis_index("tensor")

    def signal(k):
        pl.semaphore_signal(
            barrier, inc=1, device_id=dev(lax.rem(d + k, n), t), device_id_type=MESH
        )

    loop(1, n, signal)


def gather_kernel(
    n,
    t_size,
    res_ref,
    gain_ref,
    cot_ref,
    gate_ref,
    value_ref,
    state_ref,
    step_ref,
    out_ref,
    ga,
    gc,
    gw,
    a_ref,
    c_ref,
    w_ref,
    sa,
    ra,
    sc,
    rc,
    sx,
    su,
    sd,
    rw,
):
    d = lax.axis_index("dp")
    t = lax.axis_index("tensor")
    hi = d // 2
    lo = lax.rem(d, 2)
    line = n // 2
    begin = 0
    for ref in (gate_ref, value_ref, state_ref):
        w_ref[:, begin : begin + ref.shape[1]] = ref[...]
        begin += ref.shape[1]
    end = w_ref.shape[1] - out_ref.shape[1]
    w_ref[:, begin:end] = jnp.zeros((w_ref.shape[0], end - begin), BF16)
    w_ref[:, begin : begin + step_ref.shape[1]] = step_ref[...]
    w_ref[:, end:] = out_ref[...]
    parts = halves(w_ref.shape[1])
    everything = pl.ds(0, w_ref.shape[0])
    barrier = pltpu.get_barrier_semaphore()
    greet_tensor(t_size, barrier)
    greet_dp(n, barrier)
    pl.semaphore_wait(barrier, n + t_size - 2)
    mate = d + 1 - 2 * lo

    def at(h):
        return everything, parts[h]

    def own(h, sems, to):
        return push(w_ref.at[at(h)], gw.at[(d,) + at(h)], sems.at[h, d], rw.at[h, d], to, t)

    def relay(h, q, sems, to):
        return push(
            gw.at[(q,) + at(h)], gw.at[(q,) + at(h)], sems.at[h, q], rw.at[h, q], to, t
        )

    def arrive(h, q):
        push(
            gw.at[(q,) + at(h)], gw.at[(q,) + at(h)], sx.at[h, q], rw.at[h, q], mate, t
        ).wait_recv()

    has_up = hi < line - 1
    has_down = hi > 0
    own(0, sx, mate).start()

    @pl.when(has_up)
    def _():
        own(1, su, d + 2).start()
        own(0, su, d + 2).start()

    @pl.when(has_down)
    def _():
        own(1, sd, d - 2).start()
        own(0, sd, d - 2).start()

    own(1, sx, mate).start()
    res = res_ref[...]
    inv = lax.rsqrt(jnp.mean(res * res, axis=1, keepdims=True) + epsilon)
    a_ref[...] = (res * inv * gain_ref[...]).astype(BF16)
    for k in range(1, t_size):
        other = lax.rem(t + k, t_size)
        push(a_ref, ga.at[t], sa.at[other], ra.at[t], d, other).start()
    c_ref[...] = cot_ref[...].astype(BF16)
    for k in range(1, t_size):
        other = lax.rem(t + k, t_size)
        push(c_ref, gc.at[t], sc.at[other], rc.at[t], d, other).start()
    gw[d] = w_ref[...]
    ga[t] = a_ref[...]
    gc[t] = c_ref[...]
    arrive(0, mate)

    @pl.when(has_up)
    def _():
        relay(0, mate, su, d + 2).start()

    @pl.when(has_down)
    def _():
        relay(0, mate, sd, d - 2).start()

    def step(k):
        for below in (True, False):
            far = d - 2 * k if below else d + 2 * k
            far_mate = mate - 2 * k if below else mate + 2 * k
            exists = hi >= k if below else hi + k < line
            onward = jnp.logical_and(exists, has_up if below else has_down)
            sems = su if below else sd
            to = d + 2 if below else d - 2

            @pl.when(exists)
            def _():
                arrive(1, far)
                relay(1, far, sx, mate).start()

            @pl.when(onward)
            def _():
                relay(1, far, sems, to).start()

            for q in (far, far_mate):

                @pl.when(exists)
                def _():
                    arrive(0, q)

                @pl.when(onward)
                def _():
                    relay(0, q, sems, to).start()

    loop(1, line, step)
    own(0, sx, mate).wait_send()

    def finish(k):
        arrive(1, 2 * k + 1 - lo)
        relay(1, 2 * k + lo, sx, mate).wait_send()

        @pl.when(jnp.logical_and(has_up, hi >= k))
        def _():
            relay(1, 2 * k + lo, su, mate).wait_send()
            for j in range(2):
                relay(0, 2 * k + j, su, mate).wait_send()

        @pl.when(jnp.logical_and(has_down, hi <= k))
        def _():
            relay(1, 2 * k + lo, sd, mate).wait_send()
            for j in range(2):
                relay(0, 2 * k + j, sd, mate).wait_send()

    loop(0, line, finish)
    for k in range(1, t_size):
        other = lax.rem(t + k, t_size)
        push(a_ref, ga.at[other], sa.at[other], ra.at[other], d, other).wait()
        push(c_ref, gc.at[other], sc.at[other], rc.at[other], d, other).wait()


def gather_all(n, t_size, res, gain, cot, gate, value, state, step, out):
    dma = pltpu.SemaphoreType.DMA
    tok = pltpu.VMEM(res.shape, BF16)
    cols = gate.shape[1] + value.shape[1] + state.shape[1] + out.shape[1]
    cols += -(-step.shape[1] // 128) * 128
    shape = (gate.shape[0], cols)
    return pl.pallas_call(
        partial(gather_kernel, n, t_size),
        out_shape=(
            jax.ShapeDtypeStruct((t_size,) + res.shape, BF16),
            jax.ShapeDtypeStruct((t_size,) + res.shape, BF16),
            jax.ShapeDtypeStruct((n,) + shape, BF16),
        ),
        in_specs=[VM] * 8,
        out_specs=(VM, VM, VM),
        scratch_shapes=[tok, tok, pltpu.VMEM(shape, BF16)]
        + [dma((t_size,))] * 4
        + [dma((2, n))] * 4,
        compiler_params=pltpu.CompilerParams(collective_id=0, has_side_effects=True),
    )(res, gain, cot, gate, value, state, step, out)


def spread_kernel(t_size, scatter, x_ref, out_ref, ss, rs):
    d = lax.axis_index("dp")
    t = lax.axis_index("tensor")
    barrier = pltpu.get_barrier_semaphore()
    greet_tensor(t_size, barrier)
    pl.semaphore_wait(barrier, t_size - 1)
    for k in range(1, t_size):
        other = lax.rem(t + k, t_size)
        src = x_ref.at[other] if scatter else x_ref
        push(src, out_ref.at[t], ss.at[other], rs.at[t], d, other).start()
    out_ref[t] = x_ref[t] if scatter else x_ref[...]
    for k in range(1, t_size):
        other = lax.rem(t + k, t_size)
        src = x_ref.at[other] if scatter else x_ref
        push(src, out_ref.at[other], ss.at[other], rs.at[other], d, other).wait()


def spread_tensor(t_size, x, scatter, cid):
    dma = pltpu.SemaphoreType.DMA
    shape = x.shape if scatter else (t_size,) + x.shape
    return pl.pallas_call(
        partial(spread_kernel, t_size, scatter),
        out_shape=jax.ShapeDtypeStruct(shape, x.dtype),
        in_specs=[VM],
        out_specs=VM,
        scratch_shapes=[dma((t_size,))] * 2,
        compiler_params=pltpu.CompilerParams(collective_id=cid, has_side_effects=True),
    )(x)


def reduce_kernel(
    n,
    t_size,
    wa_ref,
    wb_ref,
    l_ref,
    g_ref,
    res_ref,
    gain_ref,
    cot_ref,
    sd_ref,
    st_ref,
    gate_out,
    value_out,
    state_out,
    step_out,
    proj_out,
    l_out,
    gi_out,
    norm_out,
    kv_out,
    bv_out,
    gg_out,
    sb_out,
    ld_out,
    sk_out,
    ks_out,
    bs_out,
    acc,
    rl,
    rg,
    rx0,
    rx1,
    ru1,
    rd1,
    ru0,
    rd0,
    bu1,
    bd1,
    bu0,
    bd0,
    bx1,
    st_mine,
    rst,
    st_sum,
    rst_dp,
    rsd,
    s_l,
    q_l,
    s_g,
    q_g,
    s_x0,
    q_x0,
    s_x1,
    q_x1,
    s_u1,
    q_u1,
    s_d1,
    q_d1,
    s_u0,
    q_u0,
    s_d0,
    q_d0,
    s_st,
    q_st,
    s_sp,
    q_sp,
    s_sd,
    q_sd,
):
    d = lax.axis_index("dp")
    t = lax.axis_index("tensor")
    hi = d // 2
    lo = lax.rem(d, 2)
    line = n // 2
    mate = d + 1 - 2 * lo
    barrier = pltpu.get_barrier_semaphore()
    greet_tensor(t_size, barrier)
    greet_dp(n, barrier)
    pl.semaphore_wait(barrier, n + t_size - 2)
    has_up = hi < line - 1
    has_down = hi > 0

    def send_x0(k):
        return push(
            wa_ref.at[2 * k + 1 - lo], rx0.at[k], s_x0.at[k], q_x0.at[k], mate, t
        )

    def open_x0(k):
        send_x0(line - 1 - k).start()
        send_x0(k).start()

    loop(0, line // 2, open_x0)
    if line % 2:
        send_x0(line // 2).start()

    def tensor_send(src, buf, ss, qs, other):
        return push(src.at[other], buf.at[t], ss.at[other], qs.at[t], d, other)

    for k in range(1, t_size):
        other = lax.rem(t + k, t_size)
        tensor_send(g_ref, rg, s_g, q_g, other).start()

    def sd_send(q):
        return push(sd_ref, rsd.at[d], s_sd.at[q], q_sd.at[d], q, t)

    loop(1, n, lambda k: sd_send(lax.rem(d + k, n)).start())
    for k in range(1, t_size):
        other = lax.rem(t + k, t_size)
        tensor_send(l_ref, rl, s_l, q_l, other).start()

    def hop(buf, got, ss, qs, k, to):
        return push(buf.at[k], got.at[k], ss.at[k], qs.at[k], to, t)

    def chain(k, mine, up):
        has_prev = has_down if up else has_up
        buf, got, ss, qs, to = (
            (mine[1], mine[2], mine[3], mine[4], d + 2)
            if up
            else (mine[5], mine[6], mine[7], mine[8], d - 2)
        )

        @pl.when(k > hi if up else k < hi)
        def _():
            @pl.when(has_prev)
            def _():
                hop(buf, got, ss, qs, k, to).wait_recv()
                buf[k] = (mine[0](k) + got[k].astype(F32)).astype(BF16)

            @pl.when(jnp.logical_not(has_prev))
            def _():
                buf[k] = mine[0](k).astype(BF16)

            hop(buf, got, ss, qs, k, to).start()

    def pair(k):
        return wb_ref[pl.ds(2 * k, 2)].astype(F32)

    set1 = (pair, bu1, ru1, s_u1, q_u1, bd1, rd1, s_d1, q_d1)

    def joined(k):
        return wa_ref[2 * k + lo].astype(F32) + rx0[k].astype(F32)

    set0 = (joined, bu0, ru0, s_u0, q_u0, bd0, rd0, s_d0, q_d0)

    def walk1(k):
        chain(line - 1 - k, set1, True)
        chain(k, set1, False)

    loop(0, line - 1, walk1)

    g_sum = g_ref[t].astype(F32)
    for k in range(1, t_size):
        other = lax.rem(t + k, t_size)
        push(g_ref.at[other], rg.at[other], s_g.at[other], q_g.at[other], d, other).wait()
        g_sum = g_sum + rg[other].astype(F32)
    res = res_ref[...]
    inv = lax.rsqrt(jnp.mean(res * res, axis=1, keepdims=True) + epsilon)
    unit = res * inv
    scaled = g_sum * gain_ref[...]
    inner = jnp.mean(scaled * unit, axis=1, keepdims=True)
    gi_out[...] = cot_ref[...] + inv * (scaled - unit * inner)
    st_mine[...] = st_ref[...]
    st_mine[0:1] = jnp.sum(g_sum * unit, axis=0, keepdims=True)

    def st_send(other):
        return push(st_mine, rst.at[t], s_st.at[other], q_st.at[t], d, other)

    for k in range(1, t_size):
        st_send(lax.rem(t + k, t_size)).start()

    def got_x0(k):
        push(rx0.at[k], rx0.at[k], s_x0.at[k], q_x0.at[k], mate, t).wait_recv()

    if line == 1:
        got_x0(0)
    def walk0(k):
        @pl.when(2 * k < line - 1)
        def _():
            got_x0(line - 1 - k)
            got_x0(k)

        if line % 2:

            @pl.when(2 * k == line - 1)
            def _():
                got_x0(k)

        chain(line - 1 - k, set0, True)
        chain(k, set0, False)

    loop(0, line - 1, walk0)

    proj_out[...] = wb_ref[d].astype(F32)
    bx1[...] = wb_ref[mate]

    @pl.when(has_down)
    def _():
        hop(bu1, ru1, s_u1, q_u1, hi, d).wait_recv()
        proj_out[...] = proj_out[...] + ru1[hi, lo].astype(F32)
        bx1[...] = (bx1[...].astype(F32) + ru1[hi, 1 - lo].astype(F32)).astype(BF16)

    @pl.when(has_up)
    def _():
        hop(bd1, rd1, s_d1, q_d1, hi, d).wait_recv()
        proj_out[...] = proj_out[...] + rd1[hi, lo].astype(F32)
        bx1[...] = (bx1[...].astype(F32) + rd1[hi, 1 - lo].astype(F32)).astype(BF16)

    send_x1 = push(bx1, rx1, s_x1.at[0], q_x1.at[0], mate, t)
    send_x1.start()

    st_total = st_mine[...]
    for k in range(1, t_size):
        other = lax.rem(t + k, t_size)
        push(st_mine, rst.at[other], s_st.at[other], q_st.at[other], d, other).wait()
        st_total = st_total + rst[other]
    st_sum[...] = st_total

    def sp_send(q):
        return push(st_sum, rst_dp.at[d], s_sp.at[q], q_sp.at[d], q, t)

    loop(1, n, lambda k: sp_send(lax.rem(d + k, n)).start())

    l_sum = l_ref[t].astype(F32)
    for k in range(1, t_size):
        other = lax.rem(t + k, t_size)
        push(l_ref.at[other], rl.at[other], s_l.at[other], q_l.at[other], d, other).wait()
        l_sum = l_sum + rl[other].astype(F32)
    l_out[...] = res_ref[...] + l_sum

    acc[...] = joined(hi)

    @pl.when(has_down)
    def _():
        hop(bu0, ru0, s_u0, q_u0, hi, d).wait_recv()
        acc[...] = acc[...] + ru0[hi].astype(F32)

    @pl.when(has_up)
    def _():
        hop(bd0, rd0, s_d0, q_d0, hi, d).wait_recv()
        acc[...] = acc[...] + rd0[hi].astype(F32)

    send_x1.wait()
    proj_out[...] = proj_out[...] + rx1[...].astype(F32)

    rsd[d] = sd_ref[...]
    rst_dp[d] = st_sum[...]

    def settle(k):
        q = lax.rem(d + k, n)
        push(sd_ref, rsd.at[q], s_sd.at[q], q_sd.at[q], q, t).wait()
        push(st_sum, rst_dp.at[q], s_sp.at[q], q_sp.at[q], q, t).wait()

    loop(1, n, settle)
    sums_d = jnp.sum(rsd[...], axis=0)
    sums_t = jnp.sum(rst_dp[...], axis=0)
    taps = kv_out.shape[0]
    kv_out[...] = sums_d[:taps]
    bv_out[...] = sums_d[taps : taps + 1]
    gg_out[...] = sums_d[taps + 1 : taps + 2]
    heads = step_out.shape[1]
    for i, ref in enumerate((sb_out, ld_out, sk_out)):
        ref[...] = sums_d[taps + 2 + i : taps + 3 + i, :heads]
    taps = ks_out.shape[0]
    states = ks_out.shape[1]
    norm_out[...] = sums_t[:1]
    ks_out[...] = sums_t[1 : taps + 1, :states]
    bs_out[...] = sums_t[taps + 1 : taps + 2, :states]
    begin = 0
    for ref in (gate_out, value_out, state_out, step_out):
        ref[...] = acc[:, begin : begin + ref.shape[1]]
        begin += ref.shape[1]

    def drain(k):
        send_x0(k).wait_send()

        @pl.when(k > hi)
        def _():
            hop(bu1, ru1, s_u1, q_u1, k, d).wait_send()
            hop(bu0, ru0, s_u0, q_u0, k, d).wait_send()

        @pl.when(k < hi)
        def _():
            hop(bd1, rd1, s_d1, q_d1, k, d).wait_send()
            hop(bd0, rd0, s_d0, q_d0, k, d).wait_send()

    loop(0, line, drain)


def reduce_all(n, t_size, wa, wb, l, g, res, gain, cot, small_d, small_t, dims):
    width, slice_width, heads, v_taps, s_taps, states = dims
    dma = pltpu.SemaphoreType.DMA
    vm = pltpu.VMEM
    rows, left = wa.shape[1:]
    right = wb.shape[2]
    model = res.shape[1]
    line = n // 2
    two = vm((line, 2, rows, right), BF16)
    one = vm((line, rows, left), BF16)
    tok = vm(l.shape, BF16)
    struct = jax.ShapeDtypeStruct
    t_sem = dma((t_size,))
    k_sem = dma((line,))
    n_sem = dma((n,))
    return pl.pallas_call(
        partial(reduce_kernel, n, t_size),
        out_shape=(
            struct((rows, width), F32),
            struct((rows, width), F32),
            struct((rows, slice_width), F32),
            struct((rows, heads), F32),
            struct((rows, right), F32),
            struct(res.shape, F32),
            struct(res.shape, F32),
            struct((1, model), F32),
            struct((v_taps, width), F32),
            struct((1, width), F32),
            struct((1, width), F32),
            struct((1, heads), F32),
            struct((1, heads), F32),
            struct((1, heads), F32),
            struct((s_taps, states), F32),
            struct((1, states), F32),
        ),
        in_specs=[VM] * 9,
        out_specs=(VM,) * 16,
        scratch_shapes=[
            vm((rows, left), F32),
            tok,
            tok,
            one,
            vm((rows, right), BF16),
            two,
            two,
            one,
            one,
            two,
            two,
            one,
            one,
            vm((rows, right), BF16),
            vm(small_t.shape, F32),
            vm((t_size,) + small_t.shape, F32),
            vm(small_t.shape, F32),
            vm((n,) + small_t.shape, F32),
            vm((n,) + small_d.shape, F32),
        ]
        + [t_sem] * 4
        + [k_sem] * 2
        + [dma((1,))] * 2
        + [k_sem] * 8
        + [t_sem] * 2
        + [n_sem] * 4,
        compiler_params=pltpu.CompilerParams(collective_id=3, has_side_effects=True),
    )(wa, wb, l, g, res, gain, cot, small_d, small_t)


def dot_f(a, b, dims, precision=None):
    return lax.dot_general(
        a, b, ((dims[0], dims[1]), ((), ())), preferred_element_type=F32, precision=precision
    )


def decay_of(cum_col, cum_row, allowed):
    return jnp.where(allowed, jnp.exp(jnp.where(allowed, cum_col - cum_row, 0.0)), 0.0)


def allowed_of(seg_col, seg_row):
    size = seg_col.shape[0]
    row_pos = lax.broadcasted_iota(jnp.int32, (size, size), 0)
    col_pos = lax.broadcasted_iota(jnp.int32, (size, size), 1)
    return (seg_col == seg_row) & (col_pos <= row_pos)


def pick(ref, head):
    lanes = lax.broadcasted_iota(jnp.int32, ref.shape, 1)
    return jnp.sum(jnp.where(lanes == head, ref[...], 0.0), axis=1, keepdims=True)


def mix_kernel(
    width, x_ref, b_ref, c_ref, cum_ref, cumt_ref, step_ref, skip_ref, sc_ref, sr_ref, y_ref, scores
):
    j = pl.program_id(0)
    allowed = allowed_of(sc_ref[...], sr_ref[...])

    @pl.when(j == 0)
    def _():
        scores[...] = dot_f(c_ref[...], b_ref[...], ((1,), (1,)), precise)

    count = x_ref.shape[1] // width
    for i in range(count):
        head = j * count + i
        x = x_ref[:, i * width : (i + 1) * width]
        decay = decay_of(pick(cum_ref, head), cumt_ref[pl.ds(head, 1), :], allowed)
        mixing = (scores[...] * decay).astype(BF16)
        fed = (x * pick(step_ref, head)).astype(BF16)
        y = dot_f(mixing, fed, ((1,), (0,)))
        y_ref[:, i * width : (i + 1) * width] = y + pick(skip_ref, head) * x


def mix_forward(x, b, c, cum, step, skip, seg, width):
    tokens, channels = x.shape
    pairs = channels // 128
    whole = lambda a: pl.BlockSpec(a.shape, lambda j: (0,) * a.ndim)
    block = pl.BlockSpec((tokens, 128), lambda j: (0, j))
    args = (x, b, c, cum, cum.T, step, skip[None, :], seg[:, None], seg[None, :])
    return pl.pallas_call(
        partial(mix_kernel, width),
        grid=(pairs,),
        out_shape=jax.ShapeDtypeStruct(x.shape, F32),
        in_specs=[block] + [whole(a) for a in args[1:]],
        out_specs=block,
        scratch_shapes=[pltpu.VMEM((tokens, tokens), F32)],
    )(*args)


def back_kernel(
    width,
    x_ref,
    dy_ref,
    b_ref,
    c_ref,
    cum_ref,
    cumt_ref,
    step_ref,
    skip_ref,
    sc_ref,
    sr_ref,
    dx_ref,
    db_ref,
    dc_ref,
    row_ref,
    col_ref,
    dstep_ref,
    dskip_ref,
    scores,
    d_scores,
):
    j = pl.program_id(0)
    allowed = allowed_of(sc_ref[...], sr_ref[...])

    @pl.when(j == 0)
    def _():
        scores[...] = dot_f(c_ref[...], b_ref[...], ((1,), (1,)), precise)
        d_scores[...] = jnp.zeros_like(d_scores)
        row_ref[...] = jnp.zeros_like(row_ref)
        dstep_ref[...] = jnp.zeros_like(dstep_ref)
        dskip_ref[...] = jnp.zeros_like(dskip_ref)

    lanes = lax.broadcasted_iota(jnp.int32, row_ref.shape, 1)
    count = x_ref.shape[1] // width
    for i in range(count):
        head = j * count + i
        x = x_ref[:, i * width : (i + 1) * width]
        dy = dy_ref[:, i * width : (i + 1) * width]
        step = pick(step_ref, head)
        decay = decay_of(pick(cum_ref, head), cumt_ref[pl.ds(head, 1), :], allowed)
        mixing = scores[...] * decay
        fed = (x * step).astype(BF16)
        dy_half = dy.astype(BF16)
        d_mix = dot_f(dy_half, fed, ((1,), (1,)))
        d_fed = dot_f(mixing.astype(BF16), dy_half, ((0,), (0,)))
        d_scores[...] += d_mix * decay
        energy = d_mix * mixing
        hot = lanes == head
        row_ref[...] += jnp.where(hot, jnp.sum(energy, axis=1, keepdims=True), 0.0)
        col_ref[pl.ds(head, 1), :] = jnp.sum(energy, axis=0, keepdims=True)
        dstep_ref[...] += jnp.where(hot, jnp.sum(d_fed * x, axis=1, keepdims=True), 0.0)
        dskip_ref[...] += jnp.where(hot, jnp.sum(dy * x, axis=1, keepdims=True), 0.0)
        dx_ref[:, i * width : (i + 1) * width] = d_fed * step + pick(skip_ref, head) * dy

    @pl.when(j == pl.num_programs(0) - 1)
    def _():
        grad = d_scores[...].astype(BF16)
        dc_ref[...] = dot_f(grad, b_ref[...].astype(BF16), ((1,), (0,)))
        db_ref[...] = dot_f(grad, c_ref[...].astype(BF16), ((0,), (0,)))


def mix_backward(x, dy, b, c, cum, step, skip, seg, width):
    tokens, channels = x.shape
    heads = cum.shape[1]
    pairs = channels // 128
    whole = lambda a: pl.BlockSpec(a.shape, lambda j: (0,) * a.ndim)
    block = pl.BlockSpec((tokens, 128), lambda j: (0, j))
    struct = jax.ShapeDtypeStruct
    args = (x, dy, b, c, cum, cum.T, step, skip[None, :], seg[:, None], seg[None, :])
    outs = (
        struct(x.shape, F32),
        struct(b.shape, F32),
        struct(c.shape, F32),
        struct((tokens, heads), F32),
        struct((heads, tokens), F32),
        struct((tokens, heads), F32),
        struct((tokens, heads), F32),
    )
    return pl.pallas_call(
        partial(back_kernel, width),
        grid=(pairs,),
        out_shape=outs,
        in_specs=[block, block] + [whole(a) for a in args[2:]],
        out_specs=(block,) + tuple(whole(a) for a in outs[1:]),
        scratch_shapes=[pltpu.VMEM((tokens, tokens), F32)] * 2,
    )(*args)


def conv_silu(values, kernel, shift_bias, seg_ids):
    taps = kernel.shape[0]
    length = values.shape[0]
    padded = jnp.pad(values, ((taps - 1, 0), (0, 0)))
    seg_pad = jnp.concatenate([jnp.full((taps - 1,), -1, jnp.int32), seg_ids])
    summed = jnp.zeros_like(values) + shift_bias
    for offset in range(taps):
        begin_at = taps - 1 - offset
        shifted = padded[begin_at : begin_at + length]
        same_doc = (seg_pad[begin_at : begin_at + length] == seg_ids).astype(values.dtype)
        summed = summed + kernel[offset] * shifted * same_doc[:, None]
    return jax.nn.silu(summed)


def local(
    n,
    t_size,
    residual,
    segments,
    norm_gain,
    in_gate,
    in_value,
    in_step,
    in_state,
    kernel_value,
    bias_value,
    kernel_state,
    bias_state,
    step_bias,
    log_decay,
    skip_gain,
    gate_gain,
    out_proj,
    cotangent,
):
    seg_ids = segments[0]
    width = in_gate.shape[1]
    heads = in_step.shape[1]
    states = in_state.shape[1]
    model = residual.shape[1]
    inner = width * t_size
    rows = in_gate.shape[0]
    tokens = seg_ids.shape[0]
    t = lax.axis_index("tensor")

    step_pad = -heads % 128
    full_rows, cot_full, w_full = gather_all(
        n,
        t_size,
        residual,
        norm_gain[None],
        cotangent,
        in_gate,
        in_value,
        in_state,
        in_step,
        out_proj,
    )
    full_rows = full_rows.reshape(tokens, model)
    cot_full = cot_full.reshape(tokens, model)
    w_full = w_full.reshape(model, w_full.shape[2])
    s1, s2 = 2 * width, 2 * width + states
    s3 = s2 + heads
    out_full = w_full[:, s3 + step_pad :]

    projected = jnp.dot(full_rows, w_full[:, : s3 + step_pad], preferred_element_type=F32)
    gate_raw = projected[:, :width]
    value_raw = projected[:, width:s1]
    state_raw = projected[:, s1:s2]
    step_raw = projected[:, s2:s3]
    conv_value, value_pull = jax.vjp(
        partial(conv_silu, seg_ids=seg_ids), value_raw, kernel_value, bias_value
    )
    conv_state = conv_silu(state_raw, kernel_state, bias_state, seg_ids)
    part = states // 2
    write_vec, read_vec = conv_state[:, :part], conv_state[:, part:]
    step_in = step_raw + step_bias
    step_size = jax.nn.softplus(step_in)
    rate = -jnp.exp(log_decay)
    log_keep = rate * step_size
    tri = jnp.tril(jnp.ones((tokens, tokens), F32))
    cum = jnp.dot(tri, log_keep, precision=precise)
    head_width = width // heads
    mixer_out = mix_forward(
        conv_value, write_vec, read_vec, cum, step_size, skip_gain, seg_ids, head_width
    )

    sig_gate = jax.nn.sigmoid(gate_raw)
    gate_act = gate_raw * sig_gate
    gated = mixer_out * gate_act
    grad_gate_normed = jnp.dot(cot_full, out_full, preferred_element_type=F32)
    scaled = grad_gate_normed * gate_gain
    sums = jnp.concatenate(
        [
            jnp.sum(gated * gated, axis=1).reshape(-1, 128),
            jnp.sum(scaled * gated, axis=1).reshape(-1, 128),
        ],
        axis=0,
    )
    totals = jnp.sum(spread_tensor(t_size, sums, False, 1), axis=0)
    split = tokens // 128
    total_sq = totals[:split].reshape(tokens)
    total_dot = totals[split:].reshape(tokens)
    inv_rms = lax.rsqrt(total_sq / inner + epsilon)[:, None]
    gate_normed = (gated * inv_rms * gate_gain).astype(BF16)
    grad_gate_gain = jnp.sum(grad_gate_normed * gated * inv_rms, axis=0)
    grad_gated = inv_rms * scaled - gated * inv_rms**3 * (total_dot / inner)[:, None]
    grad_mixer_out = grad_gated * gate_act
    grad_gate_raw = grad_gated * mixer_out * sig_gate * (1.0 + gate_raw * (1.0 - sig_gate))

    grad_conv_value, grad_b, grad_c, row_e, col_e, d_fed_step, d_skip = mix_backward(
        conv_value,
        grad_mixer_out,
        write_vec,
        read_vec,
        cum,
        step_size,
        skip_gain,
        seg_ids,
        head_width,
    )
    slice_width = states // t_size
    grad_bc = jnp.concatenate([grad_b, grad_c], axis=1).astype(BF16)
    pieces = grad_bc.reshape(2, tokens // 2, t_size, slice_width).transpose(2, 1, 0, 3)
    pieces = pieces.reshape(t_size, tokens // 2, 2 * slice_width)
    packed = jnp.sum(spread_tensor(t_size, pieces, True, 2).astype(F32), axis=0)
    grad_conv_state = jnp.concatenate(
        [packed[:, :slice_width], packed[:, slice_width:]], axis=0
    )
    d_keep = lax.dot_general(
        tri, row_e - col_e.T, (((0,), (0,)), ((), ())), precision=precise
    )
    grad_step_raw = (d_fed_step + d_keep * rate) * jax.nn.sigmoid(step_in)
    grad_step_bias = jnp.sum(grad_step_raw, axis=0)
    grad_log_decay = jnp.sum(d_keep * log_keep, axis=0)
    grad_skip = jnp.sum(d_skip, axis=0)

    grad_value_raw, grad_kernel_value, grad_bias_value = value_pull(grad_conv_value)
    begin = t * slice_width
    unused, state_pull = jax.vjp(
        partial(conv_silu, seg_ids=seg_ids),
        lax.dynamic_slice_in_dim(state_raw, begin, slice_width, 1),
        lax.dynamic_slice_in_dim(kernel_state, begin, slice_width, 1),
        lax.dynamic_slice_in_dim(bias_state, begin, slice_width, 0),
    )
    grad_state_slice, grad_ks, grad_bs = state_pull(grad_conv_state)
    state_cols = lax.dynamic_slice_in_dim(w_full[:, s1:s2], begin, slice_width, 1)

    fill = -(slice_width + heads) % 128
    grad_projected = jnp.concatenate(
        [
            grad_gate_raw,
            grad_value_raw,
            grad_state_slice,
            grad_step_raw,
            jnp.zeros((tokens, fill), F32),
        ],
        axis=1,
    ).astype(BF16)
    back_cat = jnp.concatenate(
        [w_full[:, :s1], state_cols, w_full[:, s2:s3], jnp.zeros((model, fill), BF16)], axis=1
    )
    grad_normed = lax.dot_general(
        grad_projected, back_cat, (((1,), (1,)), ((), ())), preferred_element_type=F32
    ).astype(BF16)
    layer_part = lax.dot_general(
        gate_normed, out_full, (((1,), (1,)), ((), ())), preferred_element_type=F32
    ).astype(BF16)
    grad_weights = lax.dot_general(
        full_rows, grad_projected, (((0,), (0,)), ((), ())), preferred_element_type=F32
    ).astype(BF16)
    grad_out = lax.dot_general(
        cot_full, gate_normed, (((0,), (0,)), ((), ())), preferred_element_type=F32
    ).astype(BF16)
    misc = jnp.stack([grad_step_bias, grad_log_decay, grad_skip])
    misc = jnp.pad(misc, ((0, 0), (0, width - heads)))
    small_d = jnp.concatenate(
        [grad_kernel_value, grad_bias_value[None], grad_gate_gain[None], misc], axis=0
    )
    small_d = jnp.pad(small_d, ((0, -small_d.shape[0] % 8), (0, 0)))
    taps = kernel_state.shape[0]
    state_grads = lax.dynamic_update_slice_in_dim(
        jnp.zeros((taps + 1, states), F32),
        jnp.concatenate([grad_ks, grad_bs[None]], axis=0),
        begin,
        1,
    )
    small_t = jnp.pad(state_grads, ((1, -(taps + 2) % 8), (0, model - states)))

    (
        sum_gate,
        sum_value,
        sum_state,
        sum_step,
        sum_out,
        layer_out,
        grad_input,
        sum_norm,
        sum_kv,
        sum_bv,
        sum_gg,
        sum_sb,
        sum_ld,
        sum_sk,
        sum_ks,
        sum_bs,
    ) = reduce_all(
        n,
        t_size,
        grad_weights.reshape(n, rows, -1),
        grad_out.reshape(n, rows, -1),
        layer_part.reshape(t_size, -1, model),
        grad_normed.reshape(t_size, -1, model),
        residual,
        norm_gain[None],
        cotangent,
        small_d,
        small_t,
        (width, slice_width, heads, kernel_value.shape[0], taps, states),
    )
    return (
        layer_out,
        grad_input,
        sum_norm[0],
        sum_gate,
        sum_value,
        sum_step,
        sum_state,
        sum_kv,
        sum_bv[0],
        sum_ks,
        sum_bs[0],
        sum_sb[0],
        sum_ld[0],
        sum_sk[0],
        sum_gg[0],
        sum_out,
    )


def solution(mesh):
    in_specs = (
        P(("dp", "tensor"), None),
        P("dp", None),
        P(),
        P("dp", "tensor"),
        P("dp", "tensor"),
        P("dp", "tensor"),
        P("dp", None),
        P(None, "tensor"),
        P("tensor"),
        P(),
        P(),
        P("tensor"),
        P("tensor"),
        P("tensor"),
        P("tensor"),
        P("dp", "tensor"),
        P(("dp", "tensor"), None),
    )
    out_specs = (
        P(("dp", "tensor"), None),
        P(("dp", "tensor"), None),
        P(),
        P("dp", "tensor"),
        P("dp", "tensor"),
        P("dp", "tensor"),
        P("dp", "tensor"),
        P(None, "tensor"),
        P("tensor"),
        P(),
        P(),
        P("tensor"),
        P("tensor"),
        P("tensor"),
        P("tensor"),
        P("dp", "tensor"),
    )
    body = partial(local, mesh.shape["dp"], mesh.shape["tensor"])
    return jax.shard_map(body, mesh=mesh, in_specs=in_specs, out_specs=out_specs, check_vma=False)
```
